512 devices in a mesh: mem: 16 (over z), sp: 32 (over x, y, core).
Axes of the slice: x: 4, y: 4, z: 16, core: 2. Of those that a mesh axis runs over, the one named last changes fastest.
Arguments:
- ensemble: bfloat16 [256, 131072], P('mem', 'sp'), may hold values from -6 to 6
- predicted: bfloat16 [256, 65536], P('mem', 'sp'), may hold values from -2 to 2
- observed: float32 [65536], P('sp'), may hold values from -6 to 6
- perturbation: bfloat16 [256, 65536], P('mem', 'sp'), may hold values from -6 to 6
- noise_variance: float32 [512], P('sp'), may hold values from 0.25 to 4
- block_lists: int32 [32, 64], P('sp'), may hold values from 0 to 511, as said below
- localization: int32 [1024, 64], P('sp'), may hold values 0 or 1
Outputs:
- increment: float32 [256, 131072], P('mem', 'sp')
The draws below stay inside these ranges and needn't reach their ends.
Inputs may be any that keep to these rules, and one draw needn't show every extreme that they name: `block_lists`: row t lists the 64 distinct data blocks used by the bricks of index t of sp, in increasing order; block j is held by index j // 16; a row uses 1 to 3 blocks of each holder, exactly 3 of some holder, and every holder gives 3 blocks to some row.
All inputs are finite; a program needn't handle non-finite values. No bound on the sum of `localization` on one device may be relied on, other than what follows from the above.
Results may differ from the reference program's by a relative error of at most 0.0055.
Values may be sent and summed in bfloat16 or wider, within the bound.
No kernel may reach another device: no remote copies, remote signals or barrier semaphores. Data moves between devices by JAX's collectives and lax.ppermute only.
A program may use at most 64 MiB of HBM per device.

```python
import math
import jax
import jax.numpy as jnp
from jax import lax

BRICK = 128
BLOCK = 128
BR_DEV = 32
DB_DEV = 16
NEED_PER = 2
CAP = 3
NEED = 64
MEMBERS = 256
BRICKS = 1024
CELLS = 131072
NBLOCKS = 512
DATA = 65536
N_SP = 32


def draw_block_lists(key, part):
    copy_count = CAP - 1
    slot_total = N_SP * copy_count
    extra_total = N_SP * (NEED_PER - 1)

    def one_row(row_key, row_index):
        first_key, second_key = jax.random.split(row_key)
        slot_holders = jnp.repeat(jnp.arange(N_SP, dtype=jnp.int32), copy_count)
        scores = jax.random.permutation(first_key, slot_total).astype(jnp.int32)
        forced = slot_holders == row_index % N_SP
        scores = jnp.where(forced, -1 - jnp.arange(slot_total, dtype=jnp.int32), scores)
        ranking = jnp.argsort(scores, stable=True)
        chosen_slots = slot_holders[ranking[:extra_total]]
        extras = jnp.sum((chosen_slots[None, :] == jnp.arange(N_SP, dtype=jnp.int32)[:, None]).astype(jnp.int32), axis=1)
        counts = 1 + extras
        segment_ends = jnp.cumsum(counts).astype(jnp.int32)
        segment_starts = segment_ends - counts
        positions = jnp.arange(NEED, dtype=jnp.int32)
        holder = jnp.sum((positions[:, None] >= segment_ends[None, :]).astype(jnp.int32), axis=1)
        slot_rank = positions - segment_starts[holder]
        holder_keys = jax.random.split(second_key, N_SP)
        shuffled = jax.vmap(lambda k: jax.random.permutation(k, DB_DEV).astype(jnp.int32))(holder_keys)
        masked = jnp.where(jnp.arange(DB_DEV, dtype=jnp.int32)[None, :] < counts[:, None], shuffled, DB_DEV)
        chosen = jnp.sort(masked, axis=1)
        return (holder * DB_DEV + chosen[holder, slot_rank]).astype(jnp.int32)
    row_keys = jax.random.split(key, N_SP)
    return jax.vmap(one_row)(row_keys, jnp.arange(N_SP, dtype=jnp.int32)).astype(jnp.int32)


def set_ends(drawn, own_key, least, top_value):
    longest = drawn.shape.index(max(drawn.shape))
    spots = []
    for shift in (0, 1):
        where = [jax.random.randint(jax.random.fold_in(own_key, axis), (), 0, length) for axis, length in enumerate(drawn.shape)]
        where[longest] = (where[longest] + shift) % drawn.shape[longest]
        spots.append(tuple(where))
    return drawn.at[spots[0]].set(least).at[spots[1]].set(top_value)


def block_levels(stream_key, dims, cuts, smallest, high):
    def one(position, parts):
        steps = jax.random.uniform(jax.random.fold_in(jax.random.fold_in(stream_key, 6), position), (parts,), jnp.float32, smallest / len(cuts), high / len(cuts))
        return jnp.repeat(jnp.exp(steps), dims[position] // parts).reshape((-1,) + (1,) * (len(dims) - position - 1))

    factor_of = one(*cuts[0])
    for cut in cuts[1:]:
        factor_of = factor_of * one(*cut)
    return factor_of


def noise(own_key, shape, spread, bound, cuts=(), kind=jnp.bfloat16):
    drawn = jax.random.normal(own_key, shape, jnp.float32) * spread
    if len(cuts) > 0:
        drawn = block_levels(own_key, shape, cuts, -0.22, 0.18) * drawn
    return jnp.clip(drawn, min=-bound, max=bound).astype(kind)


def setup_inputs(seed: int = 0) -> dict:
    key_list = jax.random.split(jax.random.key(seed), 8)
    return {
        "ensemble": noise(key_list[0], (MEMBERS, CELLS), 1.0, 6.0, ((0, 16), (1, 32))),
        "predicted": noise(key_list[1], (MEMBERS, DATA), 0.3, 2.0, ((0, 16), (1, 32))),
        "observed": noise(key_list[2], (DATA,), 1.0, 6.0, ((0, 32),), jnp.float32),
        "perturbation": noise(key_list[3], (MEMBERS, DATA), 1.0, 6.0, ((0, 16), (1, 32))),
        "noise_variance": jnp.clip(jnp.exp(math.log(4.0) - 2.7725887 * jax.random.uniform(key_list[4], (NBLOCKS,), jnp.float32) ** block_levels(key_list[4], (NBLOCKS,), ((0, 32),), -0.2, 0.2)), 0.25, 4.0),
        "block_lists": draw_block_lists(jax.random.fold_in(key_list[7], 71), 0),
        "localization": set_ends((jax.random.randint(key_list[6], (BRICKS, NEED), 0, 2) < 1).astype(jnp.int32), jax.random.fold_in(key_list[6], 1), 0, 1),
    }


def reference(ensemble, predicted, observed, perturbation, noise_variance, block_lists, localization):
    members = ensemble.shape[0]
    model_mean = lax.optimization_barrier(jnp.sum(ensemble.astype(jnp.float32), axis=0)) / members
    model_anomalies = (ensemble.astype(jnp.float32) - model_mean).astype(jnp.bfloat16)
    data_mean = lax.optimization_barrier(jnp.sum(predicted.astype(jnp.float32), axis=0)) / members
    data_anomalies = (predicted.astype(jnp.float32) - data_mean).astype(jnp.bfloat16)
    variance = jnp.repeat(noise_variance, BLOCK)
    innovation = observed[None, :] + jnp.sqrt(variance) * perturbation.astype(jnp.float32) - predicted.astype(jnp.float32)
    weighted = (innovation / variance).astype(jnp.bfloat16)
    block_total = noise_variance.shape[0]
    anomaly_blocks = data_anomalies.astype(jnp.float32).reshape(members, block_total, BLOCK)
    weighted_blocks = weighted.astype(jnp.float32).reshape(members, block_total, BLOCK)
    products = jnp.einsum('mjd,njd->jmn', anomaly_blocks, weighted_blocks).astype(jnp.bfloat16)
    flat_products = products.reshape(block_total, members * members)
    cell_share = BR_DEV * BRICK

    def per_device(device_index):
        needed = block_lists[device_index]
        needed_rows = flat_products[needed]
        pattern_rows = lax.dynamic_slice_in_dim(localization, (device_index * BR_DEV).astype(jnp.int32), BR_DEV, 0).astype(jnp.bfloat16)
        gains = jnp.dot(pattern_rows, needed_rows, preferred_element_type=jnp.float32).astype(jnp.bfloat16)
        gains = gains.reshape(BR_DEV, members, members).astype(jnp.float32)
        anomaly = lax.dynamic_slice_in_dim(model_anomalies, (device_index * cell_share).astype(jnp.int32), cell_share, 1)
        anomaly = anomaly.astype(jnp.float32).reshape(members, BR_DEV, BRICK)
        increment = jnp.einsum('bmn,mbc->nbc', gains, anomaly) / (members - 1)
        return increment.reshape(members, cell_share)
    increments = lax.map(per_device, jnp.arange(N_SP, dtype=jnp.int32))
    return jnp.transpose(increments, (1, 0, 2)).reshape(members, N_SP * cell_share)
```

```python
import jax
import jax.numpy as jnp
from jax import lax
from jax.sharding import PartitionSpec as P

SLOTS = 3


def per_device(
    ensemble, predicted, observed, perturbation, noise_variance, block_lists, localization
):
    bf16, f32 = jnp.bfloat16, jnp.float32
    mem, sp = lax.axis_size("mem"), lax.axis_size("sp")
    local = ensemble.shape[0]
    members = local * mem
    cells = ensemble.shape[1]
    bricks = localization.shape[0]
    brick = cells // bricks
    blocks = noise_variance.shape[0]
    block = predicted.shape[1] // blocks
    need = block_lists.shape[1]

    whole_ensemble = lax.all_gather(ensemble, "mem", axis=0, tiled=True)

    needed = block_lists[0]
    holder = needed // blocks
    before = jnp.sum(needed[None, :] < (holder * blocks)[:, None], axis=1)
    slot = holder * SLOTS + (jnp.arange(need) - before)
    slot_hot = slot[:, None] == jnp.arange(sp * SLOTS)[None, :]
    asked = jnp.sum(jnp.where(slot_hot, (needed % blocks)[:, None], 0), axis=0)
    asked = jnp.pad(asked.reshape(sp, SLOTS), ((0, 0), (0, 128 - SLOTS)))
    wanted = lax.all_to_all(asked, "sp", split_axis=0, concat_axis=0, tiled=True)
    wanted = wanted[:, :SLOTS].reshape(-1)
    slot_pattern = jnp.dot(
        localization.astype(bf16), slot_hot.astype(bf16), preferred_element_type=f32
    ).astype(bf16)

    cut = (blocks - 1) * block
    last = jnp.broadcast_to(predicted[None, :, cut:], (mem, local, block))
    last = lax.all_to_all(last, "mem", split_axis=0, concat_axis=0, tiled=True)
    first, wanted = lax.optimization_barrier((predicted[:, :cut], wanted))
    first = lax.all_gather(first, "mem", axis=0, tiled=True)
    whole_predicted = jnp.concatenate([first, last.reshape(members, block)], axis=1)

    data_mean = jnp.sum(whole_predicted, axis=0, dtype=f32) / members
    data_anomalies = (whole_predicted.astype(f32) - data_mean).astype(bf16)
    variance = jnp.repeat(noise_variance, block)
    innovation = (
        observed[None, :]
        + jnp.sqrt(variance) * perturbation.astype(f32)
        - predicted.astype(f32)
    )
    weighted = (innovation / variance).astype(bf16)
    products = jnp.einsum(
        "njd,mjd->jnm",
        weighted.reshape(local, blocks, block),
        data_anomalies.reshape(members, blocks, block),
        preferred_element_type=f32,
    ).astype(bf16)
    picked = (wanted[:, None] == jnp.arange(blocks)[None, :]).astype(bf16)
    sent = jnp.einsum("sj,jnm->snm", picked, products, preferred_element_type=f32).astype(bf16)
    sent = sent.reshape(sp, SLOTS * local, members)
    got = lax.all_to_all(sent, "sp", split_axis=0, concat_axis=0, tiled=True)
    got = got.reshape(sp * SLOTS, local, members)
    gains = jnp.einsum("bs,snm->bnm", slot_pattern, got, preferred_element_type=f32).astype(bf16)

    model_mean = jnp.sum(whole_ensemble, axis=0, dtype=f32) / members
    model_anomalies = (whole_ensemble.astype(f32) - model_mean).astype(bf16)
    increment = jnp.einsum(
        "bnm,mbc->nbc",
        gains,
        model_anomalies.reshape(members, bricks, brick),
        preferred_element_type=f32,
    )
    return increment.reshape(local, cells) / (members - 1)


def solution(mesh):
    in_specs = (
        P("mem", "sp"),
        P("mem", "sp"),
        P("sp"),
        P("mem", "sp"),
        P("sp"),
        P("sp", None),
        P("sp", None),
    )
    return jax.shard_map(
        per_device, mesh=mesh, in_specs=in_specs, out_specs=P("mem", "sp"), check_vma=False
    )
```

```python
import jax
import jax.numpy as jnp
from jax import lax
from jax.sharding import PartitionSpec as P

SLOTS = 3
ENSEMBLE_SCALE = 2.0**13
PREDICTED_SCALE = 2.0**14


def per_device(
    ensemble, predicted, observed, perturbation, noise_variance, block_lists, localization
):
    bf16, f16, f32 = jnp.bfloat16, jnp.float16, jnp.float32
    mem, sp = lax.axis_size("mem"), lax.axis_size("sp")
    local = ensemble.shape[0]
    members = local * mem
    cells = ensemble.shape[1]
    bricks = localization.shape[0]
    brick = cells // bricks
    blocks = noise_variance.shape[0]
    data = predicted.shape[1]
    block = data // blocks
    need = block_lists.shape[1]

    needed = block_lists[0]
    holder = needed // blocks
    before = jnp.sum(needed[None, :] < (holder * blocks)[:, None], axis=1)
    slot = holder * SLOTS + (jnp.arange(need) - before)
    slot_hot = slot[:, None] == jnp.arange(sp * SLOTS)[None, :]
    asked = jnp.sum(jnp.where(slot_hot, (needed % blocks)[:, None], 0), axis=0)
    asked = jnp.pad(asked.reshape(sp, SLOTS), ((0, 0), (0, 128 - SLOTS)))
    wanted = lax.all_to_all(asked, "sp", split_axis=0, concat_axis=0, tiled=True)
    wanted = wanted[:, :SLOTS].reshape(-1)
    slot_pattern = jnp.dot(
        localization.astype(bf16), slot_hot.astype(bf16), preferred_element_type=f32
    ).astype(bf16)

    sent = jnp.concatenate(
        [
            (predicted.astype(f32) * PREDICTED_SCALE).astype(f16),
            (ensemble.astype(f32) * ENSEMBLE_SCALE).astype(f16),
        ],
        axis=1,
    )
    whole = lax.all_gather(sent, "mem", axis=0, tiled=True)
    whole_predicted = whole[:, :data].astype(f32)
    whole_ensemble = whole[:, data:].astype(f32)

    data_mean = jnp.sum(whole_predicted, axis=0) / members
    data_anomalies = (whole_predicted - data_mean).astype(bf16)
    variance = jnp.repeat(noise_variance, block)
    innovation = (
        observed[None, :]
        + jnp.sqrt(variance) * perturbation.astype(f32)
        - predicted.astype(f32)
    )
    weighted = (innovation / variance).astype(bf16)
    products = jnp.einsum(
        "njd,mjd->jnm",
        weighted.reshape(local, blocks, block),
        data_anomalies.reshape(members, blocks, block),
        preferred_element_type=f32,
    ).astype(bf16)
    picked = (wanted[:, None] == jnp.arange(blocks)[None, :]).astype(bf16)
    chosen = jnp.einsum("sj,jnm->snm", picked, products, preferred_element_type=f32).astype(bf16)
    chosen = chosen.reshape(sp, SLOTS * local, members)
    got = lax.all_to_all(chosen, "sp", split_axis=0, concat_axis=0, tiled=True)
    got = got.reshape(sp * SLOTS, local, members)
    gains = jnp.einsum("bs,snm->bnm", slot_pattern, got, preferred_element_type=f32).astype(bf16)

    model_mean = jnp.sum(whole_ensemble, axis=0) / members
    model_anomalies = (whole_ensemble - model_mean).astype(bf16)
    increment = jnp.einsum(
        "bnm,mbc->nbc",
        gains,
        model_anomalies.reshape(members, bricks, brick),
        preferred_element_type=f32,
    )
    return increment.reshape(local, cells) / ((members - 1) * (ENSEMBLE_SCALE * PREDICTED_SCALE))


def solution(mesh):
    in_specs = (
        P("mem", "sp"),
        P("mem", "sp"),
        P("sp"),
        P("mem", "sp"),
        P("sp"),
        P("sp", None),
        P("sp", None),
    )
    return jax.shard_map(
        per_device, mesh=mesh, in_specs=in_specs, out_specs=P("mem", "sp"), check_vma=False
    )
```

```python
import jax
import jax.numpy as jnp
from jax import lax
from jax.experimental import pallas as pl
from jax.experimental.pallas import tpu as pltpu
from jax.sharding import PartitionSpec as P

SLOTS = 3
SCALE = 2.0**13


def prepare(
    predicted_ref, observed_ref, perturbation_ref, variance_ref, lists_ref, localization_ref,
    weighted_ref, asked_ref, pattern_ref,
):
    bf16, f32 = jnp.bfloat16, jnp.float32
    blocks = variance_ref.shape[1]
    block = predicted_ref.shape[1] // blocks
    for j in range(blocks):
        cut = slice(j * block, (j + 1) * block)
        variance = variance_ref[0, j]
        spread = jnp.full((1, block), variance, f32)
        innovation = (
            observed_ref[:, cut]
            + jnp.sqrt(spread) * perturbation_ref[:, cut].astype(f32)
            - predicted_ref[:, cut].astype(f32)
        )
        weighted_ref[:, cut] = (innovation / spread).astype(bf16)

    need = lists_ref.shape[1]
    holders, lanes = asked_ref.shape
    across = lists_ref[...]
    row = lax.broadcasted_iota(jnp.int32, (need, need), 0)
    column = lax.broadcasted_iota(jnp.int32, (need, need), 1)
    down = jnp.sum(jnp.where(row == column, across, 0), axis=1, keepdims=True)
    holder = lax.div(down, blocks)
    before = jnp.sum((across < holder * blocks).astype(jnp.int32), axis=1, keepdims=True)
    rank = lax.broadcasted_iota(jnp.int32, (need, 1), 0) - before
    lane = lax.broadcasted_iota(jnp.int32, (need, lanes), 1)
    ranked = jnp.where(lane == rank, down - holder * blocks, 0).astype(f32).astype(bf16)
    held = lax.div(across, blocks) == lax.broadcasted_iota(jnp.int32, (holders, need), 0)
    held = held.astype(f32).astype(bf16)
    asked = jnp.dot(held, ranked, preferred_element_type=f32)
    asked_ref[...] = asked.astype(jnp.int32)
    slot_hot = (lane == holder * SLOTS + rank).astype(f32).astype(bf16)
    uses = localization_ref[...].astype(f32).astype(bf16)
    pattern_ref[...] = jnp.dot(uses, slot_hot, preferred_element_type=f32).astype(bf16)


def per_device(
    ensemble, predicted, observed, perturbation, noise_variance, block_lists, localization
):
    bf16, f16, f32 = jnp.bfloat16, jnp.float16, jnp.float32
    mem, sp = lax.axis_size("mem"), lax.axis_size("sp")
    local = ensemble.shape[0]
    members = local * mem
    cells = ensemble.shape[1]
    bricks = localization.shape[0]
    brick = cells // bricks
    blocks = noise_variance.shape[0]
    data = predicted.shape[1]
    block = data // blocks
    slots = sp * SLOTS

    vmem = pl.BlockSpec(memory_space=pltpu.VMEM)
    weighted, asked, pattern = pl.pallas_call(
        prepare,
        out_shape=(
            jax.ShapeDtypeStruct((local, data), bf16),
            jax.ShapeDtypeStruct((sp, 128), jnp.int32),
            jax.ShapeDtypeStruct((bricks, 128), bf16),
        ),
        in_specs=[vmem, vmem, vmem, pl.BlockSpec(memory_space=pltpu.SMEM), vmem, vmem],
        out_specs=(vmem, vmem, vmem),
    )(
        predicted,
        observed.reshape(1, data),
        perturbation,
        noise_variance.reshape(1, blocks),
        block_lists,
        localization,
    )
    wanted = lax.all_to_all(asked, "sp", split_axis=0, concat_axis=0, tiled=True)
    wanted = wanted[:, :SLOTS].reshape(-1)

    sent = jnp.concatenate([predicted, ensemble], axis=1).astype(f32)
    sent = (sent * SCALE).astype(f16)
    whole = lax.all_gather(sent, "mem", axis=0, tiled=True)
    whole_predicted = whole[:, :data].astype(f32)
    whole_ensemble = whole[:, data:].astype(f32)

    data_mean = jnp.sum(whole_predicted, axis=0) / members
    data_anomalies = (whole_predicted - data_mean).astype(bf16)
    products = jnp.einsum(
        "njd,mjd->jnm",
        weighted.reshape(local, blocks, block),
        data_anomalies.reshape(members, blocks, block),
        preferred_element_type=f32,
    ).astype(bf16)
    picked = (wanted[:, None] == jnp.arange(blocks)[None, :]).astype(bf16)
    chosen = jnp.einsum("sj,jnm->snm", picked, products, preferred_element_type=f32).astype(bf16)
    chosen = chosen.reshape(sp, SLOTS * local, members)
    model_mean = jnp.sum(whole_ensemble, axis=0) / members
    chosen, model_mean, pattern = lax.optimization_barrier((chosen, model_mean, pattern))
    got = lax.all_to_all(chosen, "sp", split_axis=0, concat_axis=0, tiled=True)
    got = got.reshape(slots, local, members)
    gains = jnp.einsum(
        "bs,snm->bnm", pattern[:, :slots], got, preferred_element_type=f32
    ).astype(bf16)

    model_anomalies = (whole_ensemble - model_mean).astype(bf16)
    increment = jnp.einsum(
        "bnm,mbc->nbc",
        gains,
        model_anomalies.reshape(members, bricks, brick),
        preferred_element_type=f32,
    )
    return increment.reshape(local, cells) / ((members - 1) * SCALE**2)


def solution(mesh):
    in_specs = (
        P("mem", "sp"),
        P("mem", "sp"),
        P("sp"),
        P("mem", "sp"),
        P("sp"),
        P("sp", None),
        P("sp", None),
    )
    return jax.shard_map(
        per_device, mesh=mesh, in_specs=in_specs, out_specs=P("mem", "sp"), check_vma=False
    )
```

```python
import jax
import jax.numpy as jnp
from jax import lax
from jax.experimental import pallas as pl
from jax.experimental.pallas import tpu as pltpu
from jax.sharding import PartitionSpec as P

SCALE = 2.0**13


def prepare(
    predicted_ref, observed_ref, perturbation_ref, variance_ref, lists_ref, localization_ref,
    weighted_ref, pattern_ref,
):
    bf16, f32 = jnp.bfloat16, jnp.float32
    blocks = variance_ref.shape[1]
    block = predicted_ref.shape[1] // blocks
    for j in range(blocks):
        cut = slice(j * block, (j + 1) * block)
        spread = jnp.full((1, block), variance_ref[0, j], f32)
        innovation = (
            observed_ref[:, cut]
            + jnp.sqrt(spread) * perturbation_ref[:, cut].astype(f32)
            - predicted_ref[:, cut].astype(f32)
        )
        weighted_ref[:, cut] = (innovation / spread).astype(bf16)

    need = lists_ref.shape[1]
    row = lax.broadcasted_iota(jnp.int32, (need, need), 0)
    column = lax.broadcasted_iota(jnp.int32, (need, need), 1)
    down = jnp.sum(jnp.where(row == column, lists_ref[...], 0), axis=1, keepdims=True)
    lane = lax.broadcasted_iota(jnp.int32, (need, pattern_ref.shape[1]), 1)
    hot = (lane == down).astype(f32).astype(bf16)
    uses = localization_ref[...].astype(f32).astype(bf16)
    pattern_ref[...] = jnp.dot(uses, hot, preferred_element_type=f32).astype(bf16)


def per_device(
    ensemble, predicted, observed, perturbation, noise_variance, block_lists, localization
):
    bf16, f16, f32 = jnp.bfloat16, jnp.float16, jnp.float32
    mem, sp = lax.axis_size("mem"), lax.axis_size("sp")
    local = ensemble.shape[0]
    members = local * mem
    cells = ensemble.shape[1]
    bricks = localization.shape[0]
    brick = cells // bricks
    blocks = noise_variance.shape[0]
    data = predicted.shape[1]
    block = data // blocks

    vmem = pl.BlockSpec(memory_space=pltpu.VMEM)
    weighted, pattern = pl.pallas_call(
        prepare,
        out_shape=(
            jax.ShapeDtypeStruct((local, data), bf16),
            jax.ShapeDtypeStruct((bricks, blocks * sp), bf16),
        ),
        in_specs=[vmem, vmem, vmem, pl.BlockSpec(memory_space=pltpu.SMEM), vmem, vmem],
        out_specs=(vmem, vmem),
    )(
        predicted,
        observed.reshape(1, data),
        perturbation,
        noise_variance.reshape(1, blocks),
        block_lists,
        localization,
    )
    sent = jnp.concatenate([predicted, ensemble], axis=1).astype(f32)
    sent = (sent * SCALE).astype(f16)
    whole = lax.all_gather(sent, "mem", axis=0, tiled=True)
    whole_predicted = whole[:, :data].astype(f32)
    whole_ensemble = whole[:, data:].astype(f32)

    data_mean = jnp.sum(whole_predicted, axis=0) / members
    data_anomalies = (whole_predicted - data_mean).astype(bf16)
    products = jnp.einsum(
        "njd,mjd->jnm",
        weighted.reshape(local, blocks, block),
        data_anomalies.reshape(members, blocks, block),
        preferred_element_type=f32,
    )
    products = (products * (1 / SCALE)).astype(bf16).astype(f16)
    every = lax.all_gather(products, "sp", axis=0, tiled=True)
    gains = jnp.einsum(
        "bj,jnm->bnm", pattern, every.astype(bf16), preferred_element_type=f32
    ).astype(bf16)

    model_mean = jnp.sum(whole_ensemble, axis=0) / members
    model_anomalies = (whole_ensemble - model_mean).astype(bf16)
    increment = jnp.einsum(
        "bnm,mbc->nbc",
        gains,
        model_anomalies.reshape(members, bricks, brick),
        preferred_element_type=f32,
    )
    return increment.reshape(local, cells) / ((members - 1) * SCALE)


def solution(mesh):
    in_specs = (
        P("mem", "sp"),
        P("mem", "sp"),
        P("sp"),
        P("mem", "sp"),
        P("sp"),
        P("sp", None),
        P("sp", None),
    )
    return jax.shard_map(
        per_device, mesh=mesh, in_specs=in_specs, out_specs=P("mem", "sp"), check_vma=False
    )
```

```python
import jax
import jax.numpy as jnp
from jax import lax
from jax.experimental import pallas as pl
from jax.experimental.pallas import tpu as pltpu
from jax.sharding import PartitionSpec as P

SLOTS = 3
LISTERS = 1
SCALE = 2.0**13


def prepare(
    predicted_ref, observed_ref, perturbation_ref, variance_ref, lists_ref, localization_ref,
    weighted_ref, asked_ref, pattern_ref,
):
    bf16, f32 = jnp.bfloat16, jnp.float32
    blocks = variance_ref.shape[1]
    block = predicted_ref.shape[1] // blocks
    for j in range(blocks):
        cut = slice(j * block, (j + 1) * block)
        variance = variance_ref[0, j]
        spread = jnp.full((1, block), variance, f32)
        innovation = (
            observed_ref[:, cut]
            + jnp.sqrt(spread) * perturbation_ref[:, cut].astype(f32)
            - predicted_ref[:, cut].astype(f32)
        )
        weighted_ref[:, cut] = (innovation / spread).astype(bf16)

    need = lists_ref.shape[1]
    holders, lanes = asked_ref.shape
    across = lists_ref[...]
    row = lax.broadcasted_iota(jnp.int32, (need, need), 0)
    column = lax.broadcasted_iota(jnp.int32, (need, need), 1)
    down = jnp.sum(jnp.where(row == column, across, 0), axis=1, keepdims=True)
    holder = lax.div(down, blocks)
    before = jnp.sum((across < holder * blocks).astype(jnp.int32), axis=1, keepdims=True)
    rank = lax.broadcasted_iota(jnp.int32, (need, 1), 0) - before
    lane = lax.broadcasted_iota(jnp.int32, (need, lanes), 1)
    ranked = jnp.where(lane == rank, down - holder * blocks, 0).astype(f32).astype(bf16)
    held = lax.div(across, blocks) == lax.broadcasted_iota(jnp.int32, (holders, need), 0)
    held = held.astype(f32).astype(bf16)
    asked = jnp.dot(held, ranked, preferred_element_type=f32)
    asked_ref[...] = asked.astype(jnp.int32)
    slot_hot = (lane == holder * SLOTS + rank).astype(f32).astype(bf16)
    uses = localization_ref[...].astype(f32).astype(bf16)
    pattern_ref[...] = jnp.dot(uses, slot_hot, preferred_element_type=f32).astype(bf16)


def per_device(
    ensemble, predicted, observed, perturbation, noise_variance, block_lists, localization
):
    bf16, f16, f32 = jnp.bfloat16, jnp.float16, jnp.float32
    mem, sp = lax.axis_size("mem"), lax.axis_size("sp")
    local = ensemble.shape[0]
    members = local * mem
    cells = ensemble.shape[1]
    bricks = localization.shape[0]
    brick = cells // bricks
    blocks = noise_variance.shape[0]
    data = predicted.shape[1]
    block = data // blocks
    slots = sp * SLOTS

    vmem = pl.BlockSpec(memory_space=pltpu.VMEM)
    weighted, asked, pattern = pl.pallas_call(
        prepare,
        out_shape=(
            jax.ShapeDtypeStruct((local, data), bf16),
            jax.ShapeDtypeStruct((sp, 128), jnp.int32),
            jax.ShapeDtypeStruct((bricks, 128), bf16),
        ),
        in_specs=[vmem, vmem, vmem, pl.BlockSpec(memory_space=pltpu.SMEM), vmem, vmem],
        out_specs=(vmem, vmem, vmem),
    )(
        predicted,
        observed.reshape(1, data),
        perturbation,
        noise_variance.reshape(1, blocks),
        block_lists,
        localization,
    )
    wanted = lax.cond(
        lax.axis_index("mem") == LISTERS,
        lambda a: lax.all_to_all(a, "sp", split_axis=0, concat_axis=0, tiled=True),
        lambda a: a,
        asked,
    )
    wanted = wanted[:, :SLOTS].reshape(1, slots).astype(bf16) / blocks
    wanted = jnp.pad(wanted, ((0, local - 1), (0, -slots % 128)))
    sent = jnp.concatenate([predicted, ensemble, wanted], axis=1).astype(f32)
    sent = (sent * SCALE).astype(f16)
    whole = lax.all_gather(sent, "mem", axis=0, tiled=True)
    whole_predicted = whole[:, :data].astype(f32)
    whole_ensemble = whole[:, data : data + cells].astype(f32)
    wanted = whole[LISTERS * local, data + cells : data + cells + slots].astype(f32)

    data_mean = jnp.sum(whole_predicted, axis=0) / members
    data_anomalies = (whole_predicted - data_mean).astype(bf16)
    products = jnp.einsum(
        "njd,mjd->jnm",
        weighted.reshape(local, blocks, block),
        data_anomalies.reshape(members, blocks, block),
        preferred_element_type=f32,
    ).astype(bf16)
    picked = (wanted[:, None] == (SCALE / blocks) * jnp.arange(blocks)[None, :]).astype(bf16)
    chosen = jnp.einsum("sj,jnm->snm", picked, products, preferred_element_type=f32).astype(bf16)
    chosen = chosen.reshape(sp, SLOTS * local, members)
    model_mean = jnp.sum(whole_ensemble, axis=0) / members
    chosen, model_mean, pattern = lax.optimization_barrier((chosen, model_mean, pattern))
    got = lax.all_to_all(chosen, "sp", split_axis=0, concat_axis=0, tiled=True)
    got = got.reshape(slots, local, members)
    gains = jnp.einsum(
        "bs,snm->bnm", pattern[:, :slots], got, preferred_element_type=f32
    ).astype(bf16)

    model_anomalies = (whole_ensemble - model_mean).astype(bf16)
    increment = jnp.einsum(
        "bnm,mbc->nbc",
        gains,
        model_anomalies.reshape(members, bricks, brick),
        preferred_element_type=f32,
    )
    return increment.reshape(local, cells) / ((members - 1) * SCALE**2)


def solution(mesh):
    in_specs = (
        P("mem", "sp"),
        P("mem", "sp"),
        P("sp"),
        P("mem", "sp"),
        P("sp"),
        P("sp", None),
        P("sp", None),
    )
    return jax.shard_map(
        per_device, mesh=mesh, in_specs=in_specs, out_specs=P("mem", "sp"), check_vma=False
    )
```

```python
import jax
import jax.numpy as jnp
from jax import lax
from jax.experimental import pallas as pl
from jax.experimental.pallas import tpu as pltpu
from jax.sharding import PartitionSpec as P

SLOTS = 3
LISTERS = 1
SCALE = 2.0**13


def prepare(
    predicted_ref, ensemble_ref, observed_ref, perturbation_ref, variance_ref, lists_ref, localization_ref,
    joined_ref, weighted_ref, asked_ref, pattern_ref,
):
    bf16, f32 = jnp.bfloat16, jnp.float32
    blocks = variance_ref.shape[1]
    data = predicted_ref.shape[1]
    block = data // blocks
    joined_ref[:, :data] = predicted_ref[...]
    joined_ref[:, data:] = ensemble_ref[...]
    for j in range(blocks):
        cut = slice(j * block, (j + 1) * block)
        variance = variance_ref[0, j]
        spread = jnp.full((1, block), variance, f32)
        innovation = (
            observed_ref[:, cut]
            + jnp.sqrt(spread) * perturbation_ref[:, cut].astype(f32)
            - predicted_ref[:, cut].astype(f32)
        )
        weighted_ref[:, cut] = (innovation / spread).astype(bf16)

    need = lists_ref.shape[1]
    holders, lanes = asked_ref.shape
    across = lists_ref[...]
    row = lax.broadcasted_iota(jnp.int32, (need, need), 0)
    column = lax.broadcasted_iota(jnp.int32, (need, need), 1)
    down = jnp.sum(jnp.where(row == column, across, 0), axis=1, keepdims=True)
    holder = lax.div(down, blocks)
    before = jnp.sum((across < holder * blocks).astype(jnp.int32), axis=1, keepdims=True)
    rank = lax.broadcasted_iota(jnp.int32, (need, 1), 0) - before
    lane = lax.broadcasted_iota(jnp.int32, (need, lanes), 1)
    ranked = jnp.where(lane == rank, down - holder * blocks, 0).astype(f32).astype(bf16)
    held = lax.div(across, blocks) == lax.broadcasted_iota(jnp.int32, (holders, need), 0)
    held = held.astype(f32).astype(bf16)
    asked = jnp.dot(held, ranked, preferred_element_type=f32)
    asked_ref[...] = asked.astype(jnp.int32)
    slot_hot = (lane == holder * SLOTS + rank).astype(f32).astype(bf16)
    uses = localization_ref[...].astype(f32).astype(bf16)
    pattern_ref[...] = jnp.dot(uses, slot_hot, preferred_element_type=f32).astype(bf16)


def per_device(
    ensemble, predicted, observed, perturbation, noise_variance, block_lists, localization
):
    bf16, f16, f32 = jnp.bfloat16, jnp.float16, jnp.float32
    mem, sp = lax.axis_size("mem"), lax.axis_size("sp")
    local = ensemble.shape[0]
    members = local * mem
    cells = ensemble.shape[1]
    bricks = localization.shape[0]
    brick = cells // bricks
    blocks = noise_variance.shape[0]
    data = predicted.shape[1]
    block = data // blocks
    slots = sp * SLOTS

    vmem = pl.BlockSpec(memory_space=pltpu.VMEM)
    joined, weighted, asked, pattern = pl.pallas_call(
        prepare,
        out_shape=(
            pltpu.VMEM((local, data + cells), bf16),
            pltpu.VMEM((local, data), bf16),
            pltpu.VMEM((sp, 128), jnp.int32),
            pltpu.VMEM((bricks, 128), bf16),
        ),
        in_specs=[vmem, vmem, vmem, vmem, pl.BlockSpec(memory_space=pltpu.SMEM), vmem, vmem],
        out_specs=(vmem, vmem, vmem, vmem),
    )(
        predicted,
        ensemble,
        observed.reshape(1, data),
        perturbation,
        noise_variance.reshape(1, blocks),
        block_lists,
        localization,
    )
    wanted = lax.cond(
        lax.axis_index("mem") == LISTERS,
        lambda a: lax.all_to_all(a, "sp", split_axis=0, concat_axis=0, tiled=True),
        lambda a: a,
        asked,
    )
    wanted = wanted[:, :SLOTS].reshape(1, slots).astype(bf16) / blocks
    wanted = jnp.pad(wanted, ((0, local - 1), (0, -slots % 128)))
    sent = jnp.concatenate([joined, wanted], axis=1).astype(f32)
    sent = (sent * SCALE).astype(f16)
    whole = lax.all_gather(sent, "mem", axis=0, tiled=True)
    whole_predicted = whole[:, :data].astype(f32)
    whole_ensemble = whole[:, data : data + cells].astype(f32)
    wanted = whole[LISTERS * local, data + cells : data + cells + slots].astype(f32)

    means = jnp.sum(whole.astype(f32), axis=0) / members
    data_mean, model_mean = means[:data], means[data : data + cells]
    data_anomalies = (whole_predicted - data_mean).astype(bf16)
    products = jnp.einsum(
        "njd,mjd->jnm",
        weighted.reshape(local, blocks, block),
        data_anomalies.reshape(members, blocks, block),
        preferred_element_type=f32,
    ).astype(bf16)
    picked = (wanted[:, None] == (SCALE / blocks) * jnp.arange(blocks)[None, :]).astype(bf16)
    chosen = jnp.einsum("sj,jnm->snm", picked, products, preferred_element_type=f32).astype(bf16)
    chosen = chosen.reshape(sp, SLOTS * local, members)
    chosen, model_mean, pattern = lax.optimization_barrier((chosen, model_mean, pattern))
    got = lax.all_to_all(chosen, "sp", split_axis=0, concat_axis=0, tiled=True)
    got = got.reshape(slots, local, members)
    gains = jnp.einsum(
        "bs,snm->bnm", pattern[:, :slots], got, preferred_element_type=f32
    ).astype(bf16)

    model_anomalies = (whole_ensemble - model_mean).astype(bf16)
    increment = jnp.einsum(
        "bnm,mbc->nbc",
        gains,
        model_anomalies.reshape(members, bricks, brick),
        preferred_element_type=f32,
    )
    return increment.reshape(local, cells) / ((members - 1) * SCALE**2)


def solution(mesh):
    in_specs = (
        P("mem", "sp"),
        P("mem", "sp"),
        P("sp"),
        P("mem", "sp"),
        P("sp"),
        P("sp", None),
        P("sp", None),
    )
    return jax.shard_map(
        per_device, mesh=mesh, in_specs=in_specs, out_specs=P("mem", "sp"), check_vma=False
    )
```

```python
import jax
import jax.numpy as jnp
from jax import lax
from jax.experimental import pallas as pl
from jax.experimental.pallas import tpu as pltpu
from jax.sharding import PartitionSpec as P

SLOTS = 3
LISTERS = 2
SCALE = 2.0**13


def prepare(
    predicted_ref, ensemble_ref, observed_ref, perturbation_ref, variance_ref, lists_ref, localization_ref,
    joined_ref, weighted_ref, asked_ref, pattern_ref,
):
    bf16, f32 = jnp.bfloat16, jnp.float32
    blocks = variance_ref.shape[1]
    data = predicted_ref.shape[1]
    block = data // blocks
    joined_ref[:, :data] = predicted_ref[...]
    joined_ref[:, data:] = ensemble_ref[...]
    for j in range(blocks):
        cut = slice(j * block, (j + 1) * block)
        variance = variance_ref[0, j]
        spread = jnp.full((1, block), variance, f32)
        innovation = (
            observed_ref[:, cut]
            + jnp.sqrt(spread) * perturbation_ref[:, cut].astype(f32)
            - predicted_ref[:, cut].astype(f32)
        )
        weighted_ref[:, cut] = (innovation / spread).astype(bf16)

    need = lists_ref.shape[1]
    holders, lanes = asked_ref.shape
    across = lists_ref[...]
    row = lax.broadcasted_iota(jnp.int32, (need, need), 0)
    column = lax.broadcasted_iota(jnp.int32, (need, need), 1)
    down = jnp.sum(jnp.where(row == column, across, 0), axis=1, keepdims=True)
    holder = lax.div(down, blocks)
    before = jnp.sum((across < holder * blocks).astype(jnp.int32), axis=1, keepdims=True)
    rank = lax.broadcasted_iota(jnp.int32, (need, 1), 0) - before
    lane = lax.broadcasted_iota(jnp.int32, (need, lanes), 1)
    ranked = jnp.where(lane == rank, down - holder * blocks, 0).astype(f32).astype(bf16)
    held = lax.div(across, blocks) == lax.broadcasted_iota(jnp.int32, (holders, need), 0)
    held = held.astype(f32).astype(bf16)
    asked = jnp.dot(held, ranked, preferred_element_type=f32)
    asked_ref[...] = asked.astype(jnp.int32)
    slot_hot = (lane == holder * SLOTS + rank).astype(f32).astype(bf16)
    uses = localization_ref[...].astype(f32).astype(bf16)
    pattern_ref[...] = jnp.dot(uses, slot_hot, preferred_element_type=f32).astype(bf16)


def per_device(
    ensemble, predicted, observed, perturbation, noise_variance, block_lists, localization
):
    bf16, f16, f32 = jnp.bfloat16, jnp.float16, jnp.float32
    mem, sp = lax.axis_size("mem"), lax.axis_size("sp")
    local = ensemble.shape[0]
    members = local * mem
    cells = ensemble.shape[1]
    bricks = localization.shape[0]
    brick = cells // bricks
    blocks = noise_variance.shape[0]
    data = predicted.shape[1]
    block = data // blocks
    slots = sp * SLOTS

    vmem = pl.BlockSpec(memory_space=pltpu.VMEM)
    joined, weighted, asked, pattern = pl.pallas_call(
        prepare,
        out_shape=(
            pltpu.VMEM((local, data + cells), bf16),
            pltpu.VMEM((local, data), bf16),
            pltpu.VMEM((sp, 128), jnp.int32),
            pltpu.VMEM((bricks, 128), bf16),
        ),
        in_specs=[vmem, vmem, vmem, vmem, pl.BlockSpec(memory_space=pltpu.SMEM), vmem, vmem],
        out_specs=(vmem, vmem, vmem, vmem),
    )(
        predicted,
        ensemble,
        observed.reshape(1, data),
        perturbation,
        noise_variance.reshape(1, blocks),
        block_lists,
        localization,
    )
    wanted = lax.cond(
        lax.axis_index("mem") == LISTERS,
        lambda a: lax.all_to_all(a, "sp", split_axis=0, concat_axis=0, tiled=True),
        lambda a: a,
        asked,
    )
    wanted = wanted[:, :SLOTS].reshape(1, slots).astype(bf16) / blocks
    wanted = jnp.pad(wanted, ((0, local - 1), (0, -slots % 128)))
    sent = jnp.concatenate([joined, wanted], axis=1).astype(f32)
    sent = (sent * SCALE).astype(f16)
    whole = lax.all_gather(sent, "mem", axis=0, tiled=True)
    whole_predicted = whole[:, :data].astype(f32)
    whole_ensemble = whole[:, data : data + cells].astype(f32)
    wanted = whole[LISTERS * local, data + cells : data + cells + slots].astype(f32)

    means = jnp.sum(whole.astype(f32), axis=0) / members
    data_mean, model_mean = means[:data], means[data : data + cells]
    data_anomalies = (whole_predicted - data_mean).astype(bf16)
    products = jnp.einsum(
        "njd,mjd->jnm",
        weighted.reshape(local, blocks, block),
        data_anomalies.reshape(members, blocks, block),
        preferred_element_type=f32,
    ).astype(bf16)
    picked = (wanted[:, None] == (SCALE / blocks) * jnp.arange(blocks)[None, :]).astype(bf16)
    chosen = jnp.einsum("sj,jnm->snm", picked, products, preferred_element_type=f32).astype(bf16)
    chosen = chosen.reshape(sp, SLOTS * local, members)
    chosen, model_mean, pattern = lax.optimization_barrier((chosen, model_mean, pattern))
    got = lax.all_to_all(chosen, "sp", split_axis=0, concat_axis=0, tiled=True)
    got = got.reshape(slots, local, members)
    gains = jnp.einsum(
        "bs,snm->bnm", pattern[:, :slots], got, preferred_element_type=f32
    ).astype(bf16)

    model_anomalies = (whole_ensemble - model_mean).astype(bf16)
    increment = jnp.einsum(
        "bnm,mbc->nbc",
        gains,
        model_anomalies.reshape(members, bricks, brick),
        preferred_element_type=f32,
    )
    return increment.reshape(local, cells) / ((members - 1) * SCALE**2)


def solution(mesh):
    in_specs = (
        P("mem", "sp"),
        P("mem", "sp"),
        P("sp"),
        P("mem", "sp"),
        P("sp"),
        P("sp", None),
        P("sp", None),
    )
    return jax.shard_map(
        per_device, mesh=mesh, in_specs=in_specs, out_specs=P("mem", "sp"), check_vma=False
    )
```

```python
import jax
import jax.numpy as jnp
from jax import lax
from jax.experimental import pallas as pl
from jax.experimental.pallas import tpu as pltpu
from jax.sharding import PartitionSpec as P

SLOTS = 3
SCALE = 2.0**13


def prepare(
    predicted_ref, ensemble_ref, observed_ref, perturbation_ref, variance_ref, lists_ref, localization_ref,
    joined_ref, weighted_ref, asked_ref, pattern_ref,
):
    bf16, f32 = jnp.bfloat16, jnp.float32
    blocks = variance_ref.shape[1]
    data = predicted_ref.shape[1]
    block = data // blocks
    joined_ref[:, :data] = predicted_ref[...]
    joined_ref[:, data:] = ensemble_ref[...]
    for j in range(blocks):
        cut = slice(j * block, (j + 1) * block)
        variance = variance_ref[0, j]
        spread = jnp.full((1, block), variance, f32)
        innovation = (
            observed_ref[:, cut]
            + jnp.sqrt(spread) * perturbation_ref[:, cut].astype(f32)
            - predicted_ref[:, cut].astype(f32)
        )
        weighted_ref[:, cut] = (innovation / spread).astype(bf16)

    need = lists_ref.shape[1]
    holders, lanes = asked_ref.shape
    across = lists_ref[...]
    row = lax.broadcasted_iota(jnp.int32, (need, need), 0)
    column = lax.broadcasted_iota(jnp.int32, (need, need), 1)
    down = jnp.sum(jnp.where(row == column, across, 0), axis=1, keepdims=True)
    holder = lax.div(down, blocks)
    before = jnp.sum((across < holder * blocks).astype(jnp.int32), axis=1, keepdims=True)
    rank = lax.broadcasted_iota(jnp.int32, (need, 1), 0) - before
    lane = lax.broadcasted_iota(jnp.int32, (need, lanes), 1)
    ranked = jnp.where(lane == rank, down - holder * blocks, 0).astype(f32).astype(bf16)
    held = lax.div(across, blocks) == lax.broadcasted_iota(jnp.int32, (holders, need), 0)
    held = held.astype(f32).astype(bf16)
    asked = jnp.dot(held, ranked, preferred_element_type=f32)
    asked_ref[...] = asked.astype(jnp.int32)
    slot_hot = (lane == holder * SLOTS + rank).astype(f32).astype(bf16)
    uses = localization_ref[...].astype(f32).astype(bf16)
    pattern_ref[...] = jnp.dot(uses, slot_hot, preferred_element_type=f32).astype(bf16)


def per_device(
    ensemble, predicted, observed, perturbation, noise_variance, block_lists, localization
):
    bf16, f16, f32 = jnp.bfloat16, jnp.float16, jnp.float32
    mem, sp = lax.axis_size("mem"), lax.axis_size("sp")
    local = ensemble.shape[0]
    members = local * mem
    cells = ensemble.shape[1]
    bricks = localization.shape[0]
    brick = cells // bricks
    blocks = noise_variance.shape[0]
    data = predicted.shape[1]
    block = data // blocks
    slots = sp * SLOTS

    vmem = pl.BlockSpec(memory_space=pltpu.VMEM)
    joined, weighted, asked, pattern = pl.pallas_call(
        prepare,
        out_shape=(
            pltpu.VMEM((local, data + cells), bf16),
            pltpu.VMEM((local, data), bf16),
            pltpu.VMEM((sp, 128), jnp.int32),
            pltpu.VMEM((bricks, 128), bf16),
        ),
        in_specs=[vmem, vmem, vmem, vmem, pl.BlockSpec(memory_space=pltpu.SMEM), vmem, vmem],
        out_specs=(vmem, vmem, vmem, vmem),
    )(
        predicted,
        ensemble,
        observed.reshape(1, data),
        perturbation,
        noise_variance.reshape(1, blocks),
        block_lists,
        localization,
    )
    groups = [[m * sp + t for t in range(sp)] for m in range(mem)]
    groups[0][0], groups[1][0] = groups[1][0], groups[0][0]
    lister = (lax.axis_index("sp") == 0).astype(jnp.int32)
    wanted = lax.cond(
        lax.axis_index("mem") == lister,
        lambda a: lax.all_to_all(
            a, ("mem", "sp"), split_axis=0, concat_axis=0, tiled=True, axis_index_groups=groups
        ),
        lambda a: a,
        asked,
    )
    wanted = wanted[:, :SLOTS].reshape(1, slots).astype(bf16) / blocks
    wanted = jnp.pad(wanted, ((0, local - 1), (0, -slots % 128)))
    sent = jnp.concatenate([joined, wanted], axis=1).astype(f32)
    sent = (sent * SCALE).astype(f16)
    whole = lax.all_gather(sent, "mem", axis=0, tiled=True)
    whole_predicted = whole[:, :data].astype(f32)
    whole_ensemble = whole[:, data : data + cells].astype(f32)
    tables = whole[:, data + cells : data + cells + slots]
    wanted = jnp.where(lister == 1, tables[local], tables[0]).astype(f32)

    means = jnp.sum(whole.astype(f32), axis=0) / members
    data_mean, model_mean = means[:data], means[data : data + cells]
    data_anomalies = (whole_predicted - data_mean).astype(bf16)
    products = jnp.einsum(
        "njd,mjd->jnm",
        weighted.reshape(local, blocks, block),
        data_anomalies.reshape(members, blocks, block),
        preferred_element_type=f32,
    ).astype(bf16)
    picked = (wanted[:, None] == (SCALE / blocks) * jnp.arange(blocks)[None, :]).astype(bf16)
    chosen = jnp.einsum("sj,jnm->snm", picked, products, preferred_element_type=f32).astype(bf16)
    chosen = chosen.reshape(sp, SLOTS * local, members)
    chosen, model_mean, pattern = lax.optimization_barrier((chosen, model_mean, pattern))
    got = lax.all_to_all(chosen, "sp", split_axis=0, concat_axis=0, tiled=True)
    got = got.reshape(slots, local, members)
    gains = jnp.einsum(
        "bs,snm->bnm", pattern[:, :slots], got, preferred_element_type=f32
    ).astype(bf16)

    model_anomalies = (whole_ensemble - model_mean).astype(bf16)
    increment = jnp.einsum(
        "bnm,mbc->nbc",
        gains,
        model_anomalies.reshape(members, bricks, brick),
        preferred_element_type=f32,
    )
    return increment.reshape(local, cells) / ((members - 1) * SCALE**2)


def solution(mesh):
    in_specs = (
        P("mem", "sp"),
        P("mem", "sp"),
        P("sp"),
        P("mem", "sp"),
        P("sp"),
        P("sp", None),
        P("sp", None),
    )
    return jax.shard_map(
        per_device, mesh=mesh, in_specs=in_specs, out_specs=P("mem", "sp"), check_vma=False
    )
```

```python
import jax
import jax.numpy as jnp
from jax import lax
from jax.experimental import pallas as pl
from jax.experimental.pallas import tpu as pltpu
from jax.sharding import PartitionSpec as P

SLOTS = 3
LISTERS = 2
SCALE = 2.0**13


def prepare(
    predicted_ref, ensemble_ref, observed_ref, perturbation_ref, variance_ref, lists_ref, localization_ref,
    joined_ref, weighted_ref, asked_ref, pattern_ref,
):
    bf16, f32 = jnp.bfloat16, jnp.float32
    blocks = variance_ref.shape[1]
    data = predicted_ref.shape[1]
    block = data // blocks
    joined_ref[:, :data] = predicted_ref[...]
    joined_ref[:, data:] = ensemble_ref[...]
    for j in range(blocks):
        cut = slice(j * block, (j + 1) * block)
        variance = variance_ref[0, j]
        spread = jnp.full((1, block), variance, f32)
        innovation = (
            observed_ref[:, cut]
            + jnp.sqrt(spread) * perturbation_ref[:, cut].astype(f32)
            - predicted_ref[:, cut].astype(f32)
        )
        weighted_ref[:, cut] = (innovation / spread).astype(bf16)

    need = lists_ref.shape[1]
    holders, lanes = asked_ref.shape
    across = lists_ref[...]
    row = lax.broadcasted_iota(jnp.int32, (need, need), 0)
    column = lax.broadcasted_iota(jnp.int32, (need, need), 1)
    down = jnp.sum(jnp.where(row == column, across, 0), axis=1, keepdims=True)
    holder = lax.div(down, blocks)
    before = jnp.sum((across < holder * blocks).astype(jnp.int32), axis=1, keepdims=True)
    rank = lax.broadcasted_iota(jnp.int32, (need, 1), 0) - before
    lane = lax.broadcasted_iota(jnp.int32, (need, lanes), 1)
    ranked = jnp.where(lane == rank, down - holder * blocks, 0).astype(f32).astype(bf16)
    held = lax.div(across, blocks) == lax.broadcasted_iota(jnp.int32, (holders, need), 0)
    held = held.astype(f32).astype(bf16)
    asked = jnp.dot(held, ranked, preferred_element_type=f32)
    asked_ref[...] = asked.astype(jnp.int32)
    slot_hot = (lane == holder * SLOTS + rank).astype(f32).astype(bf16)
    uses = localization_ref[...].astype(f32).astype(bf16)
    pattern_ref[...] = jnp.dot(uses, slot_hot, preferred_element_type=f32).astype(bf16)


def per_device(
    ensemble, predicted, observed, perturbation, noise_variance, block_lists, localization
):
    bf16, f16, f32 = jnp.bfloat16, jnp.float16, jnp.float32
    mem, sp = lax.axis_size("mem"), lax.axis_size("sp")
    local = ensemble.shape[0]
    members = local * mem
    cells = ensemble.shape[1]
    bricks = localization.shape[0]
    brick = cells // bricks
    blocks = noise_variance.shape[0]
    data = predicted.shape[1]
    block = data // blocks
    slots = sp * SLOTS

    vmem = pl.BlockSpec(memory_space=pltpu.VMEM)
    joined, weighted, asked, pattern = pl.pallas_call(
        prepare,
        out_shape=(
            pltpu.VMEM((local, data + cells), bf16),
            pltpu.VMEM((local, data), bf16),
            pltpu.VMEM((sp, 128), jnp.int32),
            pltpu.VMEM((bricks, 128), bf16),
        ),
        in_specs=[vmem, vmem, vmem, vmem, pl.BlockSpec(memory_space=pltpu.SMEM), vmem, vmem],
        out_specs=(vmem, vmem, vmem, vmem),
    )(
        predicted,
        ensemble,
        observed.reshape(1, data),
        perturbation,
        noise_variance.reshape(1, blocks),
        block_lists,
        localization,
    )
    wanted = lax.cond(
        lax.axis_index("mem") == LISTERS,
        lambda a: lax.all_to_all(a, "sp", split_axis=0, concat_axis=0, tiled=True),
        lambda a: a,
        asked,
    )
    wanted = wanted[:, :SLOTS].reshape(1, slots).astype(bf16) / blocks
    wanted = jnp.pad(wanted, ((0, local - 1), (0, -slots % 128)))
    sent = jnp.concatenate([joined, wanted], axis=1).astype(f32)
    sent = (sent * SCALE).astype(f16)
    whole = lax.all_gather(sent, "mem", axis=0, tiled=True)
    whole_predicted = whole[:, :data].astype(f32)
    whole_ensemble = whole[:, data : data + cells].astype(f32)
    wanted = whole[LISTERS * local, data + cells : data + cells + slots].astype(f32)

    data_mean = jnp.sum(whole_predicted, axis=0) / members
    model_mean = jnp.sum(whole_ensemble, axis=0) / members
    data_anomalies = (whole_predicted - data_mean).astype(bf16)
    products = jnp.einsum(
        "njd,mjd->jnm",
        weighted.reshape(local, blocks, block),
        data_anomalies.reshape(members, blocks, block),
        preferred_element_type=f32,
    ).astype(bf16)
    picked = (wanted[:, None] == (SCALE / blocks) * jnp.arange(blocks)[None, :]).astype(bf16)
    chosen = jnp.einsum("sj,jnm->snm", picked, products, preferred_element_type=f32).astype(bf16)
    chosen = chosen.reshape(sp, SLOTS * local, members)
    chosen, model_mean, pattern = lax.optimization_barrier((chosen, model_mean, pattern))
    got = lax.all_to_all(chosen, "sp", split_axis=0, concat_axis=0, tiled=True)
    got = got.reshape(slots, local, members)
    gains = jnp.einsum(
        "bs,snm->bnm", pattern[:, :slots], got, preferred_element_type=f32
    ).astype(bf16)

    model_anomalies = (whole_ensemble - model_mean).astype(bf16)
    increment = jnp.einsum(
        "bnm,mbc->nbc",
        gains,
        model_anomalies.reshape(members, bricks, brick),
        preferred_element_type=f32,
    )
    return increment.reshape(local, cells) / ((members - 1) * SCALE**2)


def solution(mesh):
    in_specs = (
        P("mem", "sp"),
        P("mem", "sp"),
        P("sp"),
        P("mem", "sp"),
        P("sp"),
        P("sp", None),
        P("sp", None),
    )
    return jax.shard_map(
        per_device, mesh=mesh, in_specs=in_specs, out_specs=P("mem", "sp"), check_vma=False
    )
```
